32 devices in a mesh: grp: 2 (over x), seq: 16 (over z, y, core).
Axes of the slice: x: 2, y: 2, z: 4, core: 2. Of those that a mesh axis runs over, the one named last changes fastest.
Arguments:
- query_rows: bfloat16 [16384, 1536], P(('grp', 'seq')), parts along dimension 0, may hold values from -6 to 6
- key_rows: bfloat16 [16384, 1536], P(('grp', 'seq')), parts along dimension 0, may hold values from -6 to 6
- value_rows: bfloat16 [16384, 1536], P(('grp', 'seq')), parts along dimension 0, may hold values from -6 to 6
- doc_start: int32 [16384], P(('grp', 'seq')), parts along dimension 0, may hold values from 0 to 8191, as said below
Outputs:
- attention_out: bfloat16 [16384, 1536], P(('grp', 'seq')), parts along dimension 0
The draws below stay inside these ranges and needn't reach their ends.
There are 2 independent parts, one for each index of `grp`. The reference program is written for one: setup_inputs(seed, part) draws one part's arguments, and reference() takes and returns one part's arrays. A program takes and returns all parts, laid end to end along the dimension named above; each array names one. Nothing has to cross between parts.
Inputs may be any that keep to these rules, and one draw needn't show every extreme that they name: `doc_start`: the position of the first token of the token's document: never falling, equal to the token's own position at a document's first token and constant up to the next one.
All inputs are finite; a program needn't handle non-finite values.
Results may differ from the reference program's by a relative error of at most 0.0038.
Values may be sent and summed in bfloat16 or wider, within the bound.
A program may use at most 64 MiB of HBM per device.

```python
import math
import jax
import jax.numpy as jnp
from jax import lax

AH = 12
DH = 128
WINDOW = 2048
TOK_DEV = 512
TOKENS = 8192


def paired_rows(key):
    width = AH * DH
    query_base = jnp.clip(jax.random.normal(jax.random.fold_in(key, 11), (TOKENS, width), jnp.float32), -6.0, 6.0)
    key_base = jnp.clip(jax.random.normal(jax.random.fold_in(key, 12), (TOKENS, width), jnp.float32), -6.0, 6.0)
    return (query_base, key_base)


def draw_query_rows(key, part):
    return paired_rows(key)[0].astype(jnp.bfloat16)


def draw_key_rows(key, part):
    return paired_rows(key)[1].astype(jnp.bfloat16)


def draw_doc_start(key, part):
    shortest = 2 * TOK_DEV
    longest = min(64 * TOK_DEV, TOKENS // 2)
    doc_count = TOKENS // shortest + 1
    lengths = jax.random.randint(key, (doc_count,), shortest, longest + 1, dtype=jnp.int32)
    finish = jnp.cumsum(lengths).astype(jnp.int32)
    begins = finish - lengths
    places = jnp.arange(TOKENS, dtype=jnp.int32)
    which = jnp.searchsorted(finish, places, side='right')
    return begins[which].astype(jnp.int32)


def levels(key, extent, cuts, low, top_value):
    def one(axis_at, blocks):
        draws = jax.random.uniform(jax.random.fold_in(jax.random.fold_in(key, 6), axis_at), (blocks,), jnp.float32, low / len(cuts), top_value / len(cuts))
        return jnp.repeat(jnp.exp(draws), extent[axis_at] // blocks).reshape((-1,) + (1,) * (len(extent) - axis_at - 1))

    factor_of = one(*cuts[0])
    for cut in cuts[1:]:
        factor_of = factor_of * one(*cut)
    return factor_of


def bell_draw(own_key, extent, deviation, limit, cuts=(), kind=jnp.bfloat16):
    array = deviation * jax.random.normal(own_key, extent, jnp.float32)
    if cuts:
        array = array * levels(own_key, extent, cuts, -0.22, 0.18)
    return jnp.clip(array, -limit, limit).astype(kind)


def setup_inputs(seed: int = 0, part: int = 0) -> dict:
    seeds = jax.random.split(jax.random.key(seed), 5)
    own_keys = jax.random.split(jax.random.fold_in(seeds[4], part), 5)
    return {
        "query_rows": draw_query_rows(jax.random.fold_in(jax.random.fold_in(seeds[4], part), 71), part),
        "key_rows": draw_key_rows(jax.random.fold_in(jax.random.fold_in(seeds[4], part), 71), part),
        "value_rows": bell_draw(own_keys[2], (TOKENS, AH * DH), 1.0, 6.0, ((0, 16),)),
        "doc_start": draw_doc_start(jax.random.fold_in(jax.random.fold_in(seeds[4], part), 71), part),
    }


def attention_block(block_index, query_rows, padded_keys, padded_values, doc_start):
    first_row = (block_index * TOK_DEV).astype(jnp.int32)
    queries_here = lax.dynamic_slice_in_dim(query_rows, first_row, TOK_DEV, 0)
    keys_here = lax.dynamic_slice_in_dim(padded_keys, first_row, WINDOW + TOK_DEV, 0)
    values_here = lax.dynamic_slice_in_dim(padded_values, first_row, WINDOW + TOK_DEV, 0)
    starts = lax.dynamic_slice_in_dim(doc_start, first_row, TOK_DEV, 0)
    query_place = first_row + jnp.arange(TOK_DEV, dtype=jnp.int32)
    key_place = first_row - WINDOW + jnp.arange(WINDOW + TOK_DEV, dtype=jnp.int32)
    allowed = (key_place[None, :] <= query_place[:, None]) & (key_place[None, :] > query_place[:, None] - WINDOW) & (key_place[None, :] >= starts[:, None])
    query_heads = queries_here.reshape(TOK_DEV, AH, DH).astype(jnp.float32)
    key_heads = keys_here.reshape(WINDOW + TOK_DEV, AH, DH).astype(jnp.float32)
    value_heads = values_here.reshape(WINDOW + TOK_DEV, AH, DH).astype(jnp.float32)
    scores = jnp.einsum('qhd,khd->hqk', query_heads, key_heads) * (1.0 / math.sqrt(DH))
    scores = jnp.where(allowed[None], scores, -jnp.inf)
    largest = lax.optimization_barrier(jnp.max(scores, axis=2, keepdims=True))
    powers = jnp.exp(scores - largest)
    totals = lax.optimization_barrier(jnp.sum(powers, axis=2, keepdims=True))
    weights = powers.astype(jnp.bfloat16)
    mixed = jnp.einsum('hqk,khd->hqd', weights.astype(jnp.float32), value_heads) / totals
    return mixed.transpose(1, 0, 2).reshape(TOK_DEV, AH * DH).astype(jnp.bfloat16)

def reference(query_rows, key_rows, value_rows, doc_start):
    padding = jnp.zeros((WINDOW, AH * DH), key_rows.dtype)
    padded_keys = jnp.concatenate([padding, key_rows], axis=0)
    padded_values = jnp.concatenate([padding, value_rows], axis=0)
    blocks = jnp.arange(TOKENS // TOK_DEV, dtype=jnp.int32)
    attention_out = lax.map(lambda number: attention_block(number, query_rows, padded_keys, padded_values, doc_start), blocks)
    return attention_out.reshape(TOKENS, AH * DH)
```

```python
import functools
import math

import jax
import jax.numpy as jnp
from jax import lax
from jax.experimental import pallas as pl
from jax.experimental.pallas import tpu as pltpu
from jax.sharding import PartitionSpec as P

AH = 12
DH = 128
WINDOW = 2048
SPAN = 768
MESH = pl.DeviceIdType.MESH
HIDDEN = -1e30


def kernel(n, rows, ahead, doc_ref, q_hbm, k_hbm, v_hbm, out_ref,
           q_buf, k_buf, v_buf, low, own_sem, send_sem, recv_sem):
    group = lax.axis_index("grp")
    me = lax.axis_index("seq")
    upper = (me // 2) % 2
    odd = me % 2
    beside = me + 2 - 4 * upper
    twin = me + 1 - 2 * odd
    half = rows // 2
    sources = (k_hbm, v_hbm)
    buffers = (k_buf, v_buf)

    def columns(ref, head):
        return ref.at[:, pl.ds(pl.multiple_of(head * DH, DH), DH)]

    def slot(which, head, shard):
        return buffers[which].at[head, pl.ds(shard * rows, rows), :]

    def own_copies(head):
        pairs = [(q_hbm, q_buf.at[head])] + [(sources[w], slot(w, head, 4)) for w in (0, 1)]
        return [
            pltpu.make_async_copy(columns(source, head), target, own_sem.at[at, head])
            for at, (source, target) in enumerate(pairs)
        ]

    landing = (0, 2, 3, 1)

    def copies(kind, head, source_shard, target):
        made = []
        for w in (0, 1):
            source = columns(sources[w], head) if source_shard is None else slot(w, head, source_shard)
            made.append(pltpu.make_async_remote_copy(
                src_ref=source,
                dst_ref=slot(w, head, landing[kind]),
                send_sem=send_sem.at[kind, w, head],
                recv_sem=recv_sem.at[kind, w, head],
                device_id=(group, target),
                device_id_type=MESH,
            ))
        return made

    def begin(condition, kind, head, source_shard, target):
        @pl.when(condition)
        def _():
            for copy in copies(kind, head, source_shard, target):
                copy.start()

    def arrived(kind, head, condition):
        @pl.when(condition)
        def _():
            for copy in copies(kind, head, None, twin):
                copy.wait_recv()

    def send_own(head):
        begin(me + 4 < n, 0, head, None, me + 4)
        begin(upper == 0, 1, head, None, beside)
        begin(odd == 0, 2, head, None, twin)

    def sent(head):
        for kind, condition in (
            (0, me + 4 < n),
            (1, (upper == 0) | (me >= 4)),
            (2, (odd == 0) | (me >= 2)),
            (3, ((odd == 0) & (me >= 2)) | (me >= 5)),
        ):
            @pl.when(condition)
            def _():
                for copy in copies(kind, head, None, twin):
                    copy.wait_send()

    barrier = pltpu.get_barrier_semaphore()
    pl.semaphore_signal(barrier, inc=1, device_id=(group, beside), device_id_type=MESH)
    pl.semaphore_signal(barrier, inc=1, device_id=(group, twin), device_id_type=MESH)

    @pl.when(me >= 4)
    def _():
        pl.semaphore_signal(barrier, inc=1, device_id=(group, me - 4), device_id_type=MESH)

    @pl.when(me + 4 < n)
    def _():
        pl.semaphore_signal(barrier, inc=1, device_id=(group, me + 4), device_id_type=MESH)

    peers = 2 + (me >= 4).astype(jnp.int32) + (me + 4 < n).astype(jnp.int32)
    pl.semaphore_wait(barrier, peers)

    def first(head, carry):
        send_own(head)
        return carry

    lax.fori_loop(0, ahead, first, 0)

    def fetch(head, carry):
        for copy in own_copies(head):
            copy.start()
        return carry

    lax.fori_loop(0, AH, fetch, 0)

    for shard in range(4):
        @pl.when(me < 4 - shard)
        def _():
            def clear(head, carry):
                for buffer in buffers:
                    buffer[head, pl.ds(shard * rows, rows), :] = jnp.zeros((rows, DH), jnp.bfloat16)
                return carry

            lax.fori_loop(0, AH, clear, 0)

    row = lax.broadcasted_iota(jnp.int32, (rows, DH), 0)
    low[...] = jnp.maximum(doc_ref[...] - (me * rows - WINDOW), row + 1)

    scale = math.log2(math.e) / math.sqrt(DH)

    def attend(head):
        for part in range(2):
            span = slice(part * half, (part + 1) * half)
            queries = q_buf[head, span, :]
            lowest = low[span, 0:1]
            largest = jnp.full((half, 1), HIDDEN, jnp.float32)
            total = jnp.zeros((half, 1), jnp.float32)
            mixed = jnp.zeros((half, DH), jnp.float32)
            count = (WINDOW + half) // SPAN
            for step in range(count):
                start = part * half + step * SPAN
                keys = k_buf[head, start:start + SPAN, :]
                values = v_buf[head, start:start + SPAN, :]
                scores = lax.dot_general(
                    queries, keys, (((1,), (1,)), ((), ())), preferred_element_type=jnp.float32
                )
                place = start + lax.broadcasted_iota(jnp.int32, (half, SPAN), 1)
                allowed = place >= lowest
                if step == count - 1:
                    query = part * half + lax.broadcasted_iota(jnp.int32, (half, SPAN), 0)
                    allowed = allowed & (place <= query + WINDOW)
                scores = jnp.where(allowed, scores, HIDDEN)
                higher = jnp.maximum(largest, jnp.max(scores, axis=1, keepdims=True))
                powers = jnp.exp2((scores - higher) * scale)
                fade = jnp.exp2((largest - higher) * scale)
                total = total * fade + jnp.sum(powers, axis=1, keepdims=True)
                mixed = mixed * fade + jnp.dot(
                    powers.astype(jnp.bfloat16), values, preferred_element_type=jnp.float32
                )
                largest = higher
            out_ref[span, pl.ds(pl.multiple_of(head * DH, DH), DH)] = (mixed / total).astype(jnp.bfloat16)

    def turn(at, carry):
        @pl.when(at < AH)
        def _():
            head = at

            @pl.when(head + ahead < AH)
            def _():
                send_own(head + ahead)

            arrived(0, head, me >= 4)
            begin((upper == 1) & (me >= 4), 1, head, 0, beside)
            begin((odd == 1) & (me >= 4), 3, head, 0, twin)

        @pl.when((at >= 1) & (at < AH + 1))
        def _():
            head = at - 1
            arrived(1, head, me >= 2)
            begin((odd == 1) & (me >= 2), 2, head, 2, twin)
            begin((odd == 0) & (me >= 2), 3, head, 2, twin)

        @pl.when(at >= 2)
        def _():
            head = at - 2
            arrived(2, head, me >= 1)
            arrived(3, head, me >= 3)
            for copy in own_copies(head):
                copy.wait()
            attend(head)

        return carry

    lax.fori_loop(0, AH + 2, turn, 0)

    def finish(head, carry):
        sent(head)
        return carry

    lax.fori_loop(0, AH, finish, 0)


def local(query_rows, key_rows, value_rows, doc_start, n):
    rows = query_rows.shape[0]
    reach = WINDOW // rows + 1
    docs = jnp.broadcast_to(doc_start[:, None], (rows, DH))
    anywhere = pl.BlockSpec(memory_space=pl.ANY)
    inside = pl.BlockSpec(memory_space=pltpu.VMEM)
    return pl.pallas_call(
        functools.partial(kernel, n, rows, AH),
        out_shape=jax.ShapeDtypeStruct(query_rows.shape, jnp.bfloat16),
        in_specs=[inside, anywhere, anywhere, anywhere],
        out_specs=inside,
        scratch_shapes=[
            pltpu.VMEM((AH, rows, DH), jnp.bfloat16),
            pltpu.VMEM((AH, reach * rows, DH), jnp.bfloat16),
            pltpu.VMEM((AH, reach * rows, DH), jnp.bfloat16),
            pltpu.VMEM((rows, DH), jnp.int32),
            pltpu.SemaphoreType.DMA((3, AH)),
            pltpu.SemaphoreType.DMA((4, 2, AH)),
            pltpu.SemaphoreType.DMA((4, 2, AH)),
        ],
        compiler_params=pltpu.CompilerParams(
            collective_id=0, has_side_effects=True, vmem_limit_bytes=48 * 1024 * 1024
        ),
    )(docs, query_rows, key_rows, value_rows)


def solution(mesh):
    placed = (
        P(("grp", "seq"), None),
        P(("grp", "seq"), None),
        P(("grp", "seq"), None),
        P(("grp", "seq")),
    )
    return jax.shard_map(
        functools.partial(local, n=mesh.shape["seq"]),
        mesh=mesh, in_specs=placed, out_specs=P(("grp", "seq"), None), check_vma=False,
    )
```

```python
import functools
import math

import jax
import jax.numpy as jnp
from jax import lax
from jax.experimental import pallas as pl
from jax.experimental.pallas import tpu as pltpu
from jax.sharding import PartitionSpec as P

AH = 12
DH = 128
WINDOW = 2048
MESH = pl.DeviceIdType.MESH
HIDDEN = -1e30


def kernel(n, rows, doc_ref, q_hbm, k_hbm, v_hbm, out_ref,
           q_buf, k_buf, v_buf, low, top_buf, sum_buf, mix_buf, own_sem, send_sem, recv_sem):
    group = lax.axis_index("grp")
    me = lax.axis_index("seq")
    upper = (me // 2) % 2
    odd = me % 2
    beside = me + 2 - 4 * upper
    twin = me + 1 - 2 * odd
    half = rows // 2
    sources = (k_hbm, v_hbm)
    buffers = (k_buf, v_buf)

    def columns(ref, head):
        return ref.at[:, pl.ds(pl.multiple_of(head * DH, DH), DH)]

    def slot(which, head, shard):
        return buffers[which].at[head, pl.ds(shard * rows, rows), :]

    def own_copies(head):
        pairs = [(q_hbm, q_buf.at[head])] + [(sources[w], slot(w, head, 4)) for w in (0, 1)]
        return [
            pltpu.make_async_copy(columns(source, head), target, own_sem.at[at, head])
            for at, (source, target) in enumerate(pairs)
        ]

    landing = (0, 2, 3, 1)

    def copies(kind, head, source_shard, target, which=(0, 1)):
        made = []
        for w in which:
            source = columns(sources[w], head) if source_shard is None else slot(w, head, source_shard)
            made.append(pltpu.make_async_remote_copy(
                src_ref=source,
                dst_ref=slot(w, head, landing[kind]),
                send_sem=send_sem.at[kind, w, head],
                recv_sem=recv_sem.at[kind, w, head],
                device_id=(group, target),
                device_id_type=MESH,
            ))
        return made

    def begin(condition, kind, head, source_shard, target, which=(0, 1)):
        @pl.when(condition)
        def _():
            for copy in copies(kind, head, source_shard, target, which):
                copy.start()

    def arrived(kind, head, condition, which=(0, 1)):
        @pl.when(condition)
        def _():
            for copy in copies(kind, head, None, twin, which):
                copy.wait_recv()

    def send_own(head):
        begin(me + 4 < n, 0, head, None, me + 4)
        begin(upper == 0, 1, head, None, beside)
        begin(odd == 0, 2, head, None, twin)

    def sent(head):
        for kind, condition in (
            (0, me + 4 < n),
            (1, (upper == 0) | (me >= 4)),
            (2, (odd == 0) | (me >= 2)),
            (3, ((odd == 0) & (me >= 2)) | (me >= 5)),
        ):
            @pl.when(condition)
            def _():
                for copy in copies(kind, head, None, twin):
                    copy.wait_send()

    barrier = pltpu.get_barrier_semaphore()
    pl.semaphore_signal(barrier, inc=1, device_id=(group, beside), device_id_type=MESH)
    pl.semaphore_signal(barrier, inc=1, device_id=(group, twin), device_id_type=MESH)

    @pl.when(me >= 4)
    def _():
        pl.semaphore_signal(barrier, inc=1, device_id=(group, me - 4), device_id_type=MESH)

    @pl.when(me + 4 < n)
    def _():
        pl.semaphore_signal(barrier, inc=1, device_id=(group, me + 4), device_id_type=MESH)

    peers = 2 + (me >= 4).astype(jnp.int32) + (me + 4 < n).astype(jnp.int32)
    pl.semaphore_wait(barrier, peers)

    def first(head, carry):
        send_own(head)
        return carry

    lax.fori_loop(0, AH, first, 0)

    def fetch(head, carry):
        for copy in own_copies(head):
            copy.start()
        return carry

    lax.fori_loop(0, AH, fetch, 0)

    for shard in range(4):
        @pl.when(me < 4 - shard)
        def _():
            def clear(head, carry):
                for buffer in buffers:
                    buffer[head, pl.ds(shard * rows, rows), :] = jnp.zeros((rows, DH), jnp.bfloat16)
                return carry

            lax.fori_loop(0, AH, clear, 0)

    row = lax.broadcasted_iota(jnp.int32, (rows, DH), 0)
    starts = jnp.transpose(jnp.broadcast_to(doc_ref[...], (DH, rows)))
    low[...] = jnp.maximum(starts - (me * rows - WINDOW), row + 1)

    scale = math.log2(math.e) / math.sqrt(DH)

    def absorb(state, part, head, spans):
        span = slice(part * half, (part + 1) * half)
        queries = q_buf[head, span, :]
        lowest = low[span, 0:1]
        every = []
        for start, count in spans:
            scores = lax.dot_general(
                queries, k_buf[head, start:start + count, :], (((1,), (1,)), ((), ())),
                preferred_element_type=jnp.float32,
            )
            place = start + lax.broadcasted_iota(jnp.int32, (half, count), 1)
            allowed = place >= lowest
            if start >= WINDOW:
                query = part * half + lax.broadcasted_iota(jnp.int32, (half, count), 0)
                allowed = allowed & (place <= query + WINDOW)
            every.append(jnp.where(allowed, scores, HIDDEN))
        largest = functools.reduce(jnp.maximum, [jnp.max(x, axis=1, keepdims=True) for x in every])
        if state is not None:
            largest = jnp.maximum(largest, state[0])
        total = mixed = 0.0
        if state is not None:
            fade = jnp.exp2((state[0] - largest) * scale)
            total, mixed = state[1] * fade, state[2] * fade
        for (start, count), scores in zip(spans, every):
            powers = jnp.exp2((scores - largest) * scale)
            total = total + jnp.sum(powers, axis=1, keepdims=True)
            mixed = mixed + jnp.dot(
                powers.astype(jnp.bfloat16), v_buf[head, start:start + count, :],
                preferred_element_type=jnp.float32,
            )
        return largest, total, mixed

    def load(head, part):
        span = slice(part * half, (part + 1) * half)
        at = head % 2
        return top_buf[at, span, 0:1], sum_buf[at, span, 0:1], mix_buf[at, span, :]

    def store(head, part, state):
        span = slice(part * half, (part + 1) * half)
        at = head % 2
        top_buf[at, span, 0:1] = state[0]
        sum_buf[at, span, 0:1] = state[1]
        mix_buf[at, span, :] = state[2]

    def turn(at, carry):
        @pl.when(at < AH)
        def _():
            head = at
            for w in (0, 1):
                arrived(0, head, me >= 4, (w,))
                begin((upper == 1) & (me >= 4), 1, head, 0, beside, (w,))
                begin((odd == 1) & (me >= 4), 3, head, 0, twin, (w,))

        @pl.when(at >= 1)
        def _():
            head = at - 1
            for w in (0, 1):
                arrived(1, head, me >= 2, (w,))
                begin((odd == 1) & (me >= 2), 2, head, 2, twin, (w,))
                begin((odd == 0) & (me >= 2), 3, head, 2, twin, (w,))

        @pl.when(at < AH)
        def _():
            head = at
            for copy in own_copies(head):
                copy.wait()
            for part in (0, 1):
                store(head, part, absorb(None, part, head, (
                    (part * half, rows - part * half), (WINDOW, (part + 1) * half)
                )))

        @pl.when(at >= 1)
        def _():
            head = at - 1
            for part in (0, 1):
                store(head, part, absorb(load(head, part), part, head, ((2 * rows, rows),)))
            arrived(2, head, me >= 1)
            arrived(3, head, me >= 3)
            for part in (0, 1):
                span = slice(part * half, (part + 1) * half)
                _, total, mixed = absorb(load(head, part), part, head, ((rows, rows), (3 * rows, rows)))
                out_ref[span, pl.ds(pl.multiple_of(head * DH, DH), DH)] = (mixed / total).astype(jnp.bfloat16)

        return carry

    lax.fori_loop(0, AH + 1, turn, 0)

    def finish(head, carry):
        sent(head)
        return carry

    lax.fori_loop(0, AH, finish, 0)


def local(query_rows, key_rows, value_rows, doc_start, n):
    rows = query_rows.shape[0]
    reach = WINDOW // rows + 1
    anywhere = pl.BlockSpec(memory_space=pl.ANY)
    inside = pl.BlockSpec(memory_space=pltpu.VMEM)
    return pl.pallas_call(
        functools.partial(kernel, n, rows),
        out_shape=jax.ShapeDtypeStruct(query_rows.shape, jnp.bfloat16),
        in_specs=[inside, anywhere, anywhere, anywhere],
        out_specs=inside,
        scratch_shapes=[
            pltpu.VMEM((AH, rows, DH), jnp.bfloat16),
            pltpu.VMEM((AH, reach * rows, DH), jnp.bfloat16),
            pltpu.VMEM((AH, reach * rows, DH), jnp.bfloat16),
            pltpu.VMEM((rows, DH), jnp.int32),
            pltpu.VMEM((2, rows, DH), jnp.float32),
            pltpu.VMEM((2, rows, DH), jnp.float32),
            pltpu.VMEM((2, rows, DH), jnp.float32),
            pltpu.SemaphoreType.DMA((3, AH)),
            pltpu.SemaphoreType.DMA((4, 2, AH)),
            pltpu.SemaphoreType.DMA((4, 2, AH)),
        ],
        compiler_params=pltpu.CompilerParams(
            collective_id=0, has_side_effects=True, vmem_limit_bytes=60 * 1024 * 1024
        ),
    )(doc_start.reshape(1, rows), query_rows, key_rows, value_rows)


def solution(mesh):
    placed = (
        P(("grp", "seq"), None),
        P(("grp", "seq"), None),
        P(("grp", "seq"), None),
        P(("grp", "seq")),
    )
    return jax.shard_map(
        functools.partial(local, n=mesh.shape["seq"]),
        mesh=mesh, in_specs=placed, out_specs=P(("grp", "seq"), None), check_vma=False,
    )
```

```python
import functools
import math

import jax
import jax.numpy as jnp
from jax import lax
from jax.experimental import pallas as pl
from jax.experimental.pallas import tpu as pltpu
from jax.sharding import PartitionSpec as P

AH = 12
DH = 128
WINDOW = 2048
MESH = pl.DeviceIdType.MESH
HIDDEN = -1e30
AHEAD = 3
PIECES = (1, 1, 1, 1)


def kernel(n, rows, doc_ref, q_hbm, k_hbm, v_hbm, out_ref,
           q_buf, k_buf, v_buf, low, top_buf, sum_buf, mix_buf, own_sem, send_sem, recv_sem):
    group = lax.axis_index("grp")
    me = lax.axis_index("seq")
    upper = (me // 2) % 2
    odd = me % 2
    beside = me + 2 - 4 * upper
    twin = me + 1 - 2 * odd
    half = rows // 2
    sources = (k_hbm, v_hbm)
    buffers = (k_buf, v_buf)

    def columns(ref, head, first, count):
        return ref.at[pl.ds(first, count), pl.ds(pl.multiple_of(head * DH, DH), DH)]

    def slot(which, head, shard, first, count):
        return buffers[which].at[head, pl.ds(shard * rows + first, count), :]

    def own_copies(head):
        pairs = [(q_hbm, q_buf.at[head])] + [(sources[w], slot(w, head, 4, 0, rows)) for w in (0, 1)]
        return [
            pltpu.make_async_copy(columns(source, head, 0, rows), target, own_sem.at[at, head])
            for at, (source, target) in enumerate(pairs)
        ]

    landing = (0, 2, 3, 1)

    def copies(kind, head, source_shard, target, which=(0, 1), pieces=None):
        made = []
        count = rows // PIECES[kind]
        for w in which:
            for piece in range(PIECES[kind]) if pieces is None else pieces:
                if source_shard is None:
                    source = columns(sources[w], head, piece * count, count)
                else:
                    source = slot(w, head, source_shard, piece * count, count)
                made.append(pltpu.make_async_remote_copy(
                    src_ref=source,
                    dst_ref=slot(w, head, landing[kind], piece * count, count),
                    send_sem=send_sem.at[kind, w, piece, head],
                    recv_sem=recv_sem.at[kind, w, piece, head],
                    device_id=(group, target),
                    device_id_type=MESH,
                ))
        return made

    def begin(condition, kind, head, source_shard, target, which=(0, 1), pieces=None):
        @pl.when(condition)
        def _():
            for copy in copies(kind, head, source_shard, target, which, pieces):
                copy.start()

    def arrived(kind, head, condition, which=(0, 1), pieces=None):
        @pl.when(condition)
        def _():
            for copy in copies(kind, head, None, twin, which, pieces):
                copy.wait_recv()

    def gone(kind, head, condition):
        @pl.when(condition)
        def _():
            for copy in copies(kind, head, None, twin):
                copy.wait_send()

    def send_own(head):
        begin(me + 4 < n, 0, head, None, me + 4)
        begin(upper == 0, 1, head, None, beside)

    barrier = pltpu.get_barrier_semaphore()
    pl.semaphore_signal(barrier, inc=1, device_id=(group, beside), device_id_type=MESH)
    pl.semaphore_signal(barrier, inc=1, device_id=(group, twin), device_id_type=MESH)

    @pl.when(me >= 4)
    def _():
        pl.semaphore_signal(barrier, inc=1, device_id=(group, me - 4), device_id_type=MESH)

    @pl.when(me + 4 < n)
    def _():
        pl.semaphore_signal(barrier, inc=1, device_id=(group, me + 4), device_id_type=MESH)

    peers = 2 + (me >= 4).astype(jnp.int32) + (me + 4 < n).astype(jnp.int32)
    pl.semaphore_wait(barrier, peers)

    for head in range(AHEAD):
        send_own(head)

    def first(head, carry):
        begin(odd == 0, 2, head, None, twin)
        return carry

    lax.fori_loop(0, AH, first, 0)

    def fetch(head, carry):
        for copy in own_copies(head):
            copy.start()
        return carry

    lax.fori_loop(0, AH, fetch, 0)

    for shard in range(4):
        @pl.when(me < 4 - shard)
        def _():
            def clear(head, carry):
                for buffer in buffers:
                    buffer[head, pl.ds(shard * rows, rows), :] = jnp.zeros((rows, DH), jnp.bfloat16)
                return carry

            lax.fori_loop(0, AH, clear, 0)

    row = lax.broadcasted_iota(jnp.int32, (rows, DH), 0)
    starts = jnp.transpose(jnp.broadcast_to(doc_ref[...], (DH, rows)))
    low[...] = jnp.maximum(starts - (me * rows - WINDOW), row + 1)

    scale = math.log2(math.e) / math.sqrt(DH)

    def absorb(state, part, head, spans):
        span = slice(part * half, (part + 1) * half)
        queries = q_buf[head, span, :]
        lowest = low[span, 0:1]
        every = []
        for start, count in spans:
            scores = lax.dot_general(
                queries, k_buf[head, start:start + count, :], (((1,), (1,)), ((), ())),
                preferred_element_type=jnp.float32,
            )
            place = start + lax.broadcasted_iota(jnp.int32, (half, count), 1)
            allowed = place >= lowest
            if start >= WINDOW:
                query = part * half + lax.broadcasted_iota(jnp.int32, (half, count), 0)
                allowed = allowed & (place <= query + WINDOW)
            every.append(jnp.where(allowed, scores, HIDDEN))
        largest = functools.reduce(jnp.maximum, [jnp.max(x, axis=1, keepdims=True) for x in every])
        if state is not None:
            largest = jnp.maximum(largest, state[0])
        total = mixed = 0.0
        if state is not None:
            fade = jnp.exp2((state[0] - largest) * scale)
            total, mixed = state[1] * fade, state[2] * fade
        for (start, count), scores in zip(spans, every):
            powers = jnp.exp2((scores - largest) * scale)
            total = total + jnp.sum(powers, axis=1, keepdims=True)
            mixed = mixed + jnp.dot(
                powers.astype(jnp.bfloat16), v_buf[head, start:start + count, :],
                preferred_element_type=jnp.float32,
            )
        return largest, total, mixed

    def load(head, part):
        span = slice(part * half, (part + 1) * half)
        at = head % 2
        return top_buf[at, span, 0:1], sum_buf[at, span, 0:1], mix_buf[at, span, :]

    def store(head, part, state):
        span = slice(part * half, (part + 1) * half)
        at = head % 2
        top_buf[at, span, 0:1] = state[0]
        sum_buf[at, span, 0:1] = state[1]
        mix_buf[at, span, :] = state[2]

    def turn(at, carry):
        @pl.when(at < AH)
        def _():
            head = at
            gone(0, head, me + 4 < n)
            gone(1, head, upper == 0)

            @pl.when(head + AHEAD < AH)
            def _():
                send_own(head + AHEAD)

            for w in (0, 1):
                for piece in range(PIECES[0]):
                    arrived(0, head, me >= 4, (w,), (piece,))
                    begin((upper == 1) & (me >= 4), 1, head, 0, beside, (w,), (piece,))
                begin((odd == 1) & (me >= 4), 3, head, 0, twin, (w,))

        @pl.when(at >= 1)
        def _():
            head = at - 1
            for w in (0, 1):
                arrived(1, head, me >= 2, (w,))
                begin((odd == 1) & (me >= 2), 2, head, 2, twin, (w,))
                begin((odd == 0) & (me >= 2), 3, head, 2, twin, (w,))

        @pl.when(at < AH)
        def _():
            head = at
            for copy in own_copies(head):
                copy.wait()
            for part in (0, 1):
                store(head, part, absorb(None, part, head, (
                    (part * half, rows - part * half), (WINDOW, (part + 1) * half)
                )))

        @pl.when(at >= 1)
        def _():
            head = at - 1
            for part in (0, 1):
                store(head, part, absorb(load(head, part), part, head, ((2 * rows, rows),)))
            arrived(2, head, me >= 1)
            arrived(3, head, me >= 3)
            for part in (0, 1):
                span = slice(part * half, (part + 1) * half)
                _, total, mixed = absorb(load(head, part), part, head, ((rows, rows), (3 * rows, rows)))
                out_ref[span, pl.ds(pl.multiple_of(head * DH, DH), DH)] = (mixed / total).astype(jnp.bfloat16)

        return carry

    lax.fori_loop(0, AH + 1, turn, 0)

    def finish(head, carry):
        gone(1, head, (upper == 1) & (me >= 4))
        gone(2, head, (odd == 0) | (me >= 2))
        gone(3, head, ((odd == 0) & (me >= 2)) | (me >= 5))
        return carry

    lax.fori_loop(0, AH, finish, 0)


def local(query_rows, key_rows, value_rows, doc_start, n):
    rows = query_rows.shape[0]
    reach = WINDOW // rows + 1
    anywhere = pl.BlockSpec(memory_space=pltpu.HBM)
    inside = pl.BlockSpec(memory_space=pltpu.VMEM)
    return pl.pallas_call(
        functools.partial(kernel, n, rows),
        out_shape=jax.ShapeDtypeStruct(query_rows.shape, jnp.bfloat16),
        in_specs=[inside, anywhere, anywhere, anywhere],
        out_specs=inside,
        scratch_shapes=[
            pltpu.VMEM((AH, rows, DH), jnp.bfloat16),
            pltpu.VMEM((AH, reach * rows, DH), jnp.bfloat16),
            pltpu.VMEM((AH, reach * rows, DH), jnp.bfloat16),
            pltpu.VMEM((rows, DH), jnp.int32),
            pltpu.VMEM((2, rows, DH), jnp.float32),
            pltpu.VMEM((2, rows, DH), jnp.float32),
            pltpu.VMEM((2, rows, DH), jnp.float32),
            pltpu.SemaphoreType.DMA((3, AH)),
            pltpu.SemaphoreType.DMA((4, 2, max(PIECES), AH)),
            pltpu.SemaphoreType.DMA((4, 2, max(PIECES), AH)),
        ],
        compiler_params=pltpu.CompilerParams(
            collective_id=0, has_side_effects=True, vmem_limit_bytes=48 * 1024 * 1024
        ),
    )(doc_start.reshape(1, rows), query_rows, key_rows, value_rows)


def solution(mesh):
    placed = (
        P(("grp", "seq"), None),
        P(("grp", "seq"), None),
        P(("grp", "seq"), None),
        P(("grp", "seq")),
    )
    return jax.shard_map(
        functools.partial(local, n=mesh.shape["seq"]),
        mesh=mesh, in_specs=placed, out_specs=P(("grp", "seq"), None), check_vma=False,
    )
```

```python
import functools
import math

import jax
import jax.numpy as jnp
from jax import lax
from jax.experimental import pallas as pl
from jax.experimental.pallas import tpu as pltpu
from jax.sharding import PartitionSpec as P

AH = 12
DH = 128
WINDOW = 2048
MESH = pl.DeviceIdType.MESH
HIDDEN = -1e30
AHEAD = 3
PIECES = (1, 1, 1, 1)


def kernel(n, rows, doc_ref, q_hbm, k_hbm, v_hbm, out_ref,
           q_buf, k_buf, v_buf, low, top_buf, sum_buf, mix_buf, own_sem, send_sem, recv_sem):
    group = lax.axis_index("grp")
    me = lax.axis_index("seq")
    upper = (me // 2) % 2
    odd = me % 2
    beside = me + 2 - 4 * upper
    twin = me + 1 - 2 * odd
    half = rows // 2
    sources = (k_hbm, v_hbm)
    buffers = (k_buf, v_buf)

    def columns(ref, head, first, count):
        return ref.at[pl.ds(first, count), pl.ds(pl.multiple_of(head * DH, DH), DH)]

    def slot(which, head, shard, first, count):
        return buffers[which].at[head, pl.ds(shard * rows + first, count), :]

    def own_copies(head):
        pairs = [(q_hbm, q_buf.at[head])] + [(sources[w], slot(w, head, 4, 0, rows)) for w in (0, 1)]
        return [
            pltpu.make_async_copy(columns(source, head, 0, rows), target, own_sem.at[at, head])
            for at, (source, target) in enumerate(pairs)
        ]

    landing = (0, 2, 3, 1)

    def copies(kind, head, source_shard, target, which=(0, 1), pieces=None):
        made = []
        count = rows // PIECES[kind]
        for w in which:
            for piece in range(PIECES[kind]) if pieces is None else pieces:
                if source_shard is None:
                    source = columns(sources[w], head, piece * count, count)
                else:
                    source = slot(w, head, source_shard, piece * count, count)
                made.append(pltpu.make_async_remote_copy(
                    src_ref=source,
                    dst_ref=slot(w, head, landing[kind], piece * count, count),
                    send_sem=send_sem.at[kind, w, piece, head],
                    recv_sem=recv_sem.at[kind, w, piece, head],
                    device_id=(group, target),
                    device_id_type=MESH,
                ))
        return made

    def begin(condition, kind, head, source_shard, target, which=(0, 1), pieces=None):
        @pl.when(condition)
        def _():
            for copy in copies(kind, head, source_shard, target, which, pieces):
                copy.start()

    def arrived(kind, head, condition, which=(0, 1), pieces=None):
        @pl.when(condition)
        def _():
            for copy in copies(kind, head, None, twin, which, pieces):
                copy.wait_recv()

    def gone(kind, head, condition):
        @pl.when(condition)
        def _():
            for copy in copies(kind, head, None, twin):
                copy.wait_send()

    def send_own(head):
        begin(me + 4 < n, 0, head, None, me + 4)
        begin(upper == 0, 1, head, None, beside)
        begin(odd == 0, 2, head, None, twin)

    barrier = pltpu.get_barrier_semaphore()
    pl.semaphore_signal(barrier, inc=1, device_id=(group, beside), device_id_type=MESH)
    pl.semaphore_signal(barrier, inc=1, device_id=(group, twin), device_id_type=MESH)

    @pl.when(me >= 4)
    def _():
        pl.semaphore_signal(barrier, inc=1, device_id=(group, me - 4), device_id_type=MESH)

    @pl.when(me + 4 < n)
    def _():
        pl.semaphore_signal(barrier, inc=1, device_id=(group, me + 4), device_id_type=MESH)

    peers = 2 + (me >= 4).astype(jnp.int32) + (me + 4 < n).astype(jnp.int32)
    pl.semaphore_wait(barrier, peers)

    for head in range(AHEAD):
        send_own(head)

    def fetch(head, carry):
        for copy in own_copies(head):
            copy.start()
        return carry

    lax.fori_loop(0, AH, fetch, 0)

    for shard in range(4):
        @pl.when(me < 4 - shard)
        def _():
            def clear(head, carry):
                for buffer in buffers:
                    buffer[head, pl.ds(shard * rows, rows), :] = jnp.zeros((rows, DH), jnp.bfloat16)
                return carry

            lax.fori_loop(0, AH, clear, 0)

    row = lax.broadcasted_iota(jnp.int32, (rows, DH), 0)
    starts = jnp.transpose(jnp.broadcast_to(doc_ref[...], (DH, rows)))
    low[...] = jnp.maximum(starts - (me * rows - WINDOW), row + 1)

    scale = math.log2(math.e) / math.sqrt(DH)

    def absorb(state, part, head, spans):
        span = slice(part * half, (part + 1) * half)
        queries = q_buf[head, span, :]
        lowest = low[span, 0:1]
        every = []
        for start, count in spans:
            scores = lax.dot_general(
                queries, k_buf[head, start:start + count, :], (((1,), (1,)), ((), ())),
                preferred_element_type=jnp.float32,
            )
            place = start + lax.broadcasted_iota(jnp.int32, (half, count), 1)
            allowed = place >= lowest
            if start >= WINDOW:
                query = part * half + lax.broadcasted_iota(jnp.int32, (half, count), 0)
                allowed = allowed & (place <= query + WINDOW)
            every.append(jnp.where(allowed, scores, HIDDEN))
        largest = functools.reduce(jnp.maximum, [jnp.max(x, axis=1, keepdims=True) for x in every])
        if state is not None:
            largest = jnp.maximum(largest, state[0])
        total = mixed = 0.0
        if state is not None:
            fade = jnp.exp2((state[0] - largest) * scale)
            total, mixed = state[1] * fade, state[2] * fade
        for (start, count), scores in zip(spans, every):
            powers = jnp.exp2((scores - largest) * scale)
            total = total + jnp.sum(powers, axis=1, keepdims=True)
            mixed = mixed + jnp.dot(
                powers.astype(jnp.bfloat16), v_buf[head, start:start + count, :],
                preferred_element_type=jnp.float32,
            )
        return largest, total, mixed

    def load(head, part):
        span = slice(part * half, (part + 1) * half)
        at = head % 2
        return top_buf[at, span, 0:1], sum_buf[at, span, 0:1], mix_buf[at, span, :]

    def store(head, part, state):
        span = slice(part * half, (part + 1) * half)
        at = head % 2
        top_buf[at, span, 0:1] = state[0]
        sum_buf[at, span, 0:1] = state[1]
        mix_buf[at, span, :] = state[2]

    def turn(at, carry):
        @pl.when(at < AH)
        def _():
            head = at
            gone(0, head, me + 4 < n)
            gone(1, head, upper == 0)

            @pl.when(head + AHEAD < AH)
            def _():
                send_own(head + AHEAD)

            for w in (0, 1):
                for piece in range(PIECES[0]):
                    arrived(0, head, me >= 4, (w,), (piece,))
                    begin((upper == 1) & (me >= 4), 1, head, 0, beside, (w,), (piece,))
                begin((odd == 1) & (me >= 4), 3, head, 0, twin, (w,))

        @pl.when(at >= 1)
        def _():
            head = at - 1
            for w in (0, 1):
                arrived(1, head, me >= 2, (w,))
                begin((odd == 1) & (me >= 2), 2, head, 2, twin, (w,))
                begin((odd == 0) & (me >= 2), 3, head, 2, twin, (w,))

        @pl.when(at < AH)
        def _():
            head = at
            for copy in own_copies(head):
                copy.wait()
            for part in (0, 1):
                store(head, part, absorb(None, part, head, (
                    (part * half, rows - part * half), (WINDOW, (part + 1) * half)
                )))

        @pl.when(at >= 1)
        def _():
            head = at - 1
            for part in (0, 1):
                store(head, part, absorb(load(head, part), part, head, ((2 * rows, rows),)))
            arrived(2, head, me >= 1)
            arrived(3, head, me >= 3)
            for part in (0, 1):
                span = slice(part * half, (part + 1) * half)
                _, total, mixed = absorb(load(head, part), part, head, ((rows, rows), (3 * rows, rows)))
                out_ref[span, pl.ds(pl.multiple_of(head * DH, DH), DH)] = (mixed / total).astype(jnp.bfloat16)

        return carry

    lax.fori_loop(0, AH + 1, turn, 0)

    def finish(head, carry):
        gone(1, head, (upper == 1) & (me >= 4))
        gone(2, head, (odd == 0) | (me >= 2))
        gone(3, head, ((odd == 0) & (me >= 2)) | (me >= 5))
        return carry

    lax.fori_loop(0, AH, finish, 0)


def local(query_rows, key_rows, value_rows, doc_start, n):
    rows = query_rows.shape[0]
    reach = WINDOW // rows + 1
    anywhere = pl.BlockSpec(memory_space=pltpu.HBM)
    inside = pl.BlockSpec(memory_space=pltpu.VMEM)
    return pl.pallas_call(
        functools.partial(kernel, n, rows),
        out_shape=jax.ShapeDtypeStruct(query_rows.shape, jnp.bfloat16),
        in_specs=[inside, anywhere, anywhere, anywhere],
        out_specs=inside,
        scratch_shapes=[
            pltpu.VMEM((AH, rows, DH), jnp.bfloat16),
            pltpu.VMEM((AH, reach * rows, DH), jnp.bfloat16),
            pltpu.VMEM((AH, reach * rows, DH), jnp.bfloat16),
            pltpu.VMEM((rows, DH), jnp.int32),
            pltpu.VMEM((2, rows, DH), jnp.float32),
            pltpu.VMEM((2, rows, DH), jnp.float32),
            pltpu.VMEM((2, rows, DH), jnp.float32),
            pltpu.SemaphoreType.DMA((3, AH)),
            pltpu.SemaphoreType.DMA((4, 2, max(PIECES), AH)),
            pltpu.SemaphoreType.DMA((4, 2, max(PIECES), AH)),
        ],
        compiler_params=pltpu.CompilerParams(
            collective_id=0, has_side_effects=True, vmem_limit_bytes=48 * 1024 * 1024
        ),
    )(doc_start.reshape(1, rows), query_rows, key_rows, value_rows)


def solution(mesh):
    placed = (
        P(("grp", "seq"), None),
        P(("grp", "seq"), None),
        P(("grp", "seq"), None),
        P(("grp", "seq")),
    )
    return jax.shard_map(
        functools.partial(local, n=mesh.shape["seq"]),
        mesh=mesh, in_specs=placed, out_specs=P(("grp", "seq"), None), check_vma=False,
    )
```
